32 devices in a mesh: outer: 4 (over y, core), seq: 8 (over z, x).
Axes of the slice: x: 2, y: 2, z: 4, core: 2. Of those that a mesh axis runs over, the one named last changes fastest.
Arguments:
- tokens: bfloat16 [32768, 640], P(('outer', 'seq')), may hold values from -6 to 6
- lengths: int32 [4, 64], P('outer'), may hold values from 1 to 4096, 7936 in all within a row
- gain_attn: float32 [640], replicated, may hold values from 0.5 to 1.5
- w_query: bfloat16 [640, 1024], replicated, may hold values from -0.25 to 0.25
- w_keyvalue: bfloat16 [640, 512], replicated, may hold values from -0.25 to 0.25
- w_out: bfloat16 [1024, 640], replicated, may hold values from -1.5 to 1.5
- gain_ffn: float32 [640], replicated, may hold values from 0.5 to 1.5
- w_gate_up: bfloat16 [640, 4096], replicated, may hold values from -0.25 to 0.25
- w_down: bfloat16 [2048, 640], replicated, may hold values from -0.125 to 0.125
- cotangent: bfloat16 [32768, 640], P(('outer', 'seq')), may hold values from -6 to 6
Outputs:
- mixed: bfloat16 [32768, 640], P(('outer', 'seq'))
- input_grad: float32 [32768, 640], P(('outer', 'seq'))
- shared_kv: bfloat16 [32768, 512], P(('outer', 'seq'))
- grad_gain_attn: float32 [640], replicated
- grad_w_query: float32 [640, 1024], replicated
- grad_w_keyvalue: float32 [640, 512], replicated
- grad_w_out: float32 [1024, 640], replicated
- grad_gain_ffn: float32 [640], replicated
- grad_w_gate_up: float32 [640, 4096], replicated
- grad_w_down: float32 [2048, 640], replicated
The draws below stay inside these ranges and needn't reach their ends.
Inputs may be any that keep to these rules, and one draw needn't show every extreme that they name: Each row of lengths holds 64 positive lengths that sum to 7936; the largest in each row is exactly 4096.
All inputs are finite; a program needn't handle non-finite values.
Results may differ from the reference program's by a relative error of at most 0.012.
Values may be sent and summed in bfloat16 or wider, within the bound.
No kernel may reach another device: no remote copies, remote signals or barrier semaphores. Data moves between devices by JAX's collectives and lax.ppermute only.
A program may use at most 192 MiB of HBM per device.

```python
import math
import jax
import jax.numpy as jnp
import numpy as np
from jax import lax

D = 640
HEADS = 4
HEAD = 256
FF = 2048
WINDOW = 512
DOCS = 64
SEQ_TOK = 8192
LIVE = 7936
LONGEST = 4096
TOKENS = 32768
N_OUTER = 4


def steps_of(stream_key, dims, split, least, largest):
    gain, own = 1.0, jax.random.fold_in(stream_key, 6)
    for axis_at, blocks in split:
        steps = jnp.exp(jax.random.uniform(jax.random.fold_in(own, axis_at), (blocks,), jnp.float32, least / len(split), largest / len(split)))
        gain = gain * jnp.repeat(steps, dims[axis_at] // blocks).reshape([-1 if axis == axis_at else 1 for axis in range(len(dims))])
    return gain


def length_profile(number_of, total, bound, skew):
    portions = [(1 << 20) // math.isqrt(grade ** skew) + 1 for grade in range(2, number_of + 1)]
    surplus, counts = total - bound - (number_of - 1), [1] * (number_of - 1)
    while surplus > 0:
        free = [i for i in range(number_of - 1) if counts[i] < bound]
        whole, remaining = sum([portions[i] for i in free]), surplus
        for i in free:
            more = min(bound - counts[i], max(1, remaining * portions[i] // whole), surplus)
            counts[i] = counts[i] + more
            surplus = surplus - more
    return np.array([bound] + counts)


def uneven(stream_key, count, total, bound, lean):
    if count == 2:
        one = jax.random.randint(stream_key, (), max(1, total - bound), min(bound, total - 1) + 1)
        return jnp.stack([one, total - one])
    tallies = jnp.asarray(length_profile(count, total, bound, lean), jnp.int32)
    pairs = (count - 1) // 2
    source_of, taker = tallies[1:1 + 2 * pairs:2], tallies[2:2 + 2 * pairs:2]
    slack = jnp.minimum(source_of - 1, bound - taker)
    moved = jax.random.randint(jax.random.fold_in(stream_key, 1), (pairs,), 0, 1 << 20) % (slack + 1)
    tallies = tallies.at[1:1 + 2 * pairs:2].set(source_of - moved).at[2:2 + 2 * pairs:2].set(taker + moved)
    return tallies[jax.random.permutation(jax.random.fold_in(stream_key, 2), count)]


def centred(key, shape, scale, most, pieces=(), kind=jnp.bfloat16):
    values = scale * jax.random.normal(key, shape, jnp.float32)
    if pieces:
        values = values * steps_of(key, shape, pieces, -0.22, 0.18)
    return jnp.clip(values, -most, most).astype(kind)


def setup_inputs(seed: int = 0) -> dict:
    splits = jax.random.split(jax.random.key(seed), 11)
    tokens = centred(splits[0], (TOKENS, D), 1.0, 6.0, ((0, 32),))
    lengths = jax.vmap(lambda own: uneven(own, DOCS, LIVE, LONGEST, 2))(jax.random.split(splits[1], N_OUTER)).reshape((N_OUTER, DOCS)).astype(jnp.int32)
    gain_attn = jnp.clip(1.0 + 0.1 * jax.random.normal(splits[2], (D,), jnp.float32), 0.5, 1.5)
    w_query = centred(splits[3], (D, HEADS * HEAD), D ** -0.5, 0.25)
    w_keyvalue = centred(splits[4], (D, 2 * HEAD), D ** -0.5, 0.25)
    w_out = centred(splits[5], (HEADS * HEAD, D), (max(2, HEADS * HEAD // 64)) ** -0.5, 1.5)
    gain_ffn = jnp.clip(1.0 + 0.1 * jax.random.normal(splits[6], (D,), jnp.float32), 0.5, 1.5)
    w_gate_up = centred(splits[7], (D, 2 * FF), D ** -0.5, 0.25)
    w_down = centred(splits[8], (FF, D), FF ** -0.5, 0.125)
    cotangent = centred(splits[9], (TOKENS, D), 1.0, 6.0, ((0, 32),))
    return {"tokens": tokens, "lengths": lengths, "gain_attn": gain_attn, "w_query": w_query, "w_keyvalue": w_keyvalue, "w_out": w_out, "gain_ffn": gain_ffn, "w_gate_up": w_gate_up, "w_down": w_down, "cotangent": cotangent}


EPS = 1e-06

@jax.custom_vjp
def low(v):
    return lax.optimization_barrier(v.astype(jnp.bfloat16)).astype(jnp.float32)

@jax.custom_vjp
def low_back(v):
    return v

def low_keep(v):
    return (low(v), None)

def low_pass(kept, grad):
    return (grad,)

def back_keep(v):
    return (v, None)

def back_low(kept, grad):
    return (low(grad),)
low.defvjp(low_keep, low_pass)
low_back.defvjp(back_keep, back_low)

def doc_places(length_row, positions):
    doc_ends = jnp.cumsum(length_row)
    passed = positions[:, None] >= doc_ends[None, :]
    segment = lax.optimization_barrier(jnp.sum(passed.astype(jnp.int32), axis=1))
    doc_start = lax.optimization_barrier(jnp.sum(jnp.where(passed, length_row[None, :], 0), axis=1))
    segment = jnp.where(positions < 0, -1, segment)
    return (segment, positions - doc_start)

def angles(places, head_size):
    half_size = head_size // 2
    frequency = jnp.exp(jnp.arange(half_size, dtype=jnp.float32) * (-2.0 * math.log(10000.0) / head_size))
    angle_table = places.astype(jnp.float32)[:, None] * frequency[None, :]
    return (jnp.cos(angle_table), jnp.sin(angle_table))

def rotate(vector, cos_table, sin_table, turn_sign):
    half_size = vector.shape[-1] // 2
    front_half = vector[..., :half_size]
    back_half = vector[..., half_size:]
    return jnp.concatenate([front_half * cos_table - turn_sign * back_half * sin_table, back_half * cos_table + turn_sign * front_half * sin_table], axis=-1)

def normalize(vector, gain_vec):
    return vector * lax.rsqrt(lax.optimization_barrier(jnp.mean(vector * vector, axis=-1, keepdims=True)) + EPS) * gain_vec

def project(left_side, right_side):
    return jnp.dot(left_side, right_side, precision=lax.Precision.HIGHEST, preferred_element_type=jnp.float32)

def attention(queries, keys, values, segments):
    per_group = SEQ_TOK // WINDOW
    padded_keys = jnp.pad(keys.reshape(N_OUTER, SEQ_TOK, HEAD), ((0, 0), (WINDOW, 0), (0, 0)))
    padded_values = jnp.pad(values.reshape(N_OUTER, SEQ_TOK, HEAD), ((0, 0), (WINDOW, 0), (0, 0)))
    padded_seg = jnp.pad(segments.reshape(N_OUTER, SEQ_TOK), ((0, 0), (WINDOW, 0)), constant_values=-1)
    within = jnp.arange(WINDOW, dtype=jnp.int32)
    across = jnp.arange(2 * WINDOW, dtype=jnp.int32)
    band_mask = (across[None, :] > within[:, None]) & (across[None, :] <= within[:, None] + WINDOW)

    def one_block(block_index):
        group_index = (block_index // per_group).astype(jnp.int32)
        first_row = (block_index % per_group * WINDOW).astype(jnp.int32)
        query_block = lax.dynamic_slice_in_dim(queries, block_index * WINDOW, WINDOW, 0)
        seg_query = lax.dynamic_slice_in_dim(segments, block_index * WINDOW, WINDOW, 0)
        key_block = lax.dynamic_slice(padded_keys, (group_index, first_row, jnp.int32(0)), (1, 2 * WINDOW, HEAD))[0]
        value_block = lax.dynamic_slice(padded_values, (group_index, first_row, jnp.int32(0)), (1, 2 * WINDOW, HEAD))[0]
        key_segment_ids = lax.dynamic_slice(padded_seg, (group_index, first_row), (1, 2 * WINDOW))[0]
        allowed = (seg_query[:, None] == key_segment_ids[None, :]) & band_mask
        raw_scores = low_back(jnp.einsum('qhd,kd->hqk', query_block, key_block, precision=lax.Precision.HIGHEST) * HEAD ** (-0.5))
        scores = jnp.where(allowed[None], raw_scores, -1e+30)
        row_top = lax.optimization_barrier(jnp.max(scores, axis=-1, keepdims=True))
        exp_scores = jnp.exp(scores - row_top)
        probs = exp_scores / lax.optimization_barrier(jnp.sum(exp_scores, axis=-1, keepdims=True))
        return jnp.einsum('hqk,kd->qhd', low(probs), value_block, precision=lax.Precision.HIGHEST)
    block_out = lax.map(jax.checkpoint(one_block), jnp.arange(TOKENS // WINDOW, dtype=jnp.int32))
    return block_out.reshape(TOKENS, HEADS * HEAD)

def forward(hidden_in, gain_attn, w_query, w_keyvalue, w_out, gain_ffn, w_gate_up, w_down, segments, places, live_rows):
    cos_table, sin_table = angles(places, HEAD)
    normed_attn = low(normalize(hidden_in, gain_attn))
    query_pre = low_back(project(normed_attn, w_query))
    pair_pre = low_back(project(normed_attn, w_keyvalue))
    queries = low(rotate(query_pre.reshape(TOKENS, HEADS, HEAD), cos_table[:, None, :], sin_table[:, None, :], 1.0))
    keys = low(rotate(pair_pre[:, :HEAD], cos_table, sin_table, 1.0))
    values = low(pair_pre[:, HEAD:])
    context = low(low_back(attention(queries, keys, values, segments)))
    hidden_mid = hidden_in + low_back(project(context, w_out))
    normed_ffn = low(normalize(hidden_mid, gain_ffn))
    gate_up = low_back(project(normed_ffn, w_gate_up))
    gate_part = gate_up[:, :FF]
    activated = low(gate_part * jax.nn.sigmoid(gate_part) * gate_up[:, FF:])
    result = (hidden_mid + low_back(project(activated, w_down))) * live_rows
    return (result, jnp.concatenate([keys, values], axis=1))

def reference(tokens, lengths, gain_attn, w_query, w_keyvalue, w_out, gain_ffn, w_gate_up, w_down, cotangent):
    positions = jnp.arange(SEQ_TOK, dtype=jnp.int32)
    seg_rows, place_rows = jax.vmap(lambda length_row: doc_places(length_row, positions))(lengths)
    segments = seg_rows.reshape(TOKENS)
    places = place_rows.reshape(TOKENS)
    live_rows = (segments < DOCS).astype(jnp.float32)[:, None]

    def run(hidden_in, gain_one, query_mat, pair_mat, out_mat, gain_two, gate_mat, down_mat):
        return forward(hidden_in, gain_one, query_mat, pair_mat, out_mat, gain_two, gate_mat, down_mat, segments, places, live_rows)
    result, pullback, shared = jax.vjp(run, tokens.astype(jnp.float32), gain_attn.astype(jnp.float32), w_query.astype(jnp.float32), w_keyvalue.astype(jnp.float32), w_out.astype(jnp.float32), gain_ffn.astype(jnp.float32), w_gate_up.astype(jnp.float32), w_down.astype(jnp.float32), has_aux=True)
    grads = pullback(cotangent.astype(jnp.float32))
    return (result.astype(jnp.bfloat16), grads[0], shared.astype(jnp.bfloat16), grads[1], grads[2], grads[3], grads[4], grads[5], grads[6], grads[7])
```

```python
import functools
import math

import jax
import jax.numpy as jnp
from jax import lax
from jax.experimental import pallas as pl
from jax.experimental.pallas import tpu as pltpu
from jax.sharding import Mesh
from jax.sharding import PartitionSpec as P

WINDOW = 512
TILE = 256
SPAN = WINDOW + TILE
HB = 256
EPS = 1e-06
BF = jnp.bfloat16
F32 = jnp.float32
VMEM = 58 * 2**20


def dot(a, b, ca, cb, precision=None):
    return lax.dot_general(
        a, b, (((ca,), (cb,)), ((), ())), precision=precision, preferred_element_type=F32
    )


def sds(shape, dtype):
    return jax.ShapeDtypeStruct(shape, dtype)


def whole(shape):
    return pl.BlockSpec(shape, lambda *_: (0,) * len(shape))


def anywhere():
    return pl.BlockSpec(memory_space=pl.ANY)


def call(kernel, name, grid, ins, outs, out_shape, scratch=(), scalars=0, aliases=None, flops=0, nbytes=0):
    return pl.pallas_call(
        kernel,
        name=name,
        grid_spec=pltpu.PrefetchScalarGridSpec(
            num_scalar_prefetch=scalars,
            grid=grid,
            in_specs=ins,
            out_specs=outs,
            scratch_shapes=list(scratch),
        ),
        out_shape=out_shape,
        input_output_aliases=aliases or {},
        compiler_params=pltpu.CompilerParams(vmem_limit_bytes=VMEM),
        cost_estimate=pl.CostEstimate(
            flops=int(flops), bytes_accessed=int(nbytes), transcendentals=0
        ),
    )


def pre_kernel(first, tok, lens, gain, wkv, normed_o, kv_o, tail_o, cos_o, sin_o, meta_o):
    step = pl.program_id(0)
    docs = lens.shape[1]
    half = cos_o.shape[1]
    rows_i = lax.broadcasted_iota(jnp.int32, (docs, docs), 0)
    cols_i = lax.broadcasted_iota(jnp.int32, (docs, docs), 1)
    upto = (rows_i <= cols_i).astype(F32)
    lens8 = jnp.broadcast_to(lens[...].astype(F32), (8, docs))
    ends = dot(lens8, upto, 1, 0, lax.Precision.HIGHEST)[0:1]
    pos = (
        lax.broadcasted_iota(jnp.int32, (TILE, 1), 0) + (first[0] + step * TILE)
    ).astype(F32)
    passed = pos >= ends
    seg = jnp.sum(jnp.where(passed, 1.0, 0.0), axis=1, keepdims=True)
    start = jnp.max(jnp.where(passed, ends, 0.0), axis=1, keepdims=True)
    live = jnp.where(seg < docs, 1.0, 0.0)
    low = jnp.maximum(start, pos - (WINDOW - 1.0))
    frequency = jnp.exp(
        lax.broadcasted_iota(jnp.int32, (1, half), 1).astype(F32)
        * (-2.0 * math.log(10000.0) / (2 * half))
    )
    angle = (pos - start) * frequency
    cos = jnp.cos(angle)
    sin = jnp.sin(angle)
    cos_o[...] = cos
    sin_o[...] = sin
    x = tok[...].astype(F32)
    root = lax.rsqrt(jnp.mean(x * x, axis=1, keepdims=True) + EPS)
    normed = (x * root * gain[...]).astype(BF)
    normed_o[...] = normed
    lane = lax.broadcasted_iota(jnp.int32, (TILE, 128), 1)
    meta_o[...] = jnp.where(lane == 0, root, jnp.where(lane == 1, live, low))
    pair = dot(normed, wkv[...], 1, 0)
    a, b = pair[:, :half], pair[:, half : 2 * half]
    kv = jnp.concatenate([a * cos - b * sin, b * cos + a * sin, pair[:, 2 * half :]], axis=1)
    kv = kv.astype(BF)
    kv_o[...] = kv
    tail_o[...] = kv


def attend_kernel(base, heads, head, *refs):
    (first, normed, tok, cos_r, sin_r, meta, prev, cur, wq, wo, gain) = refs[:11]
    (q_o, p_o, ctx_o, mid_o, nf_o, win) = refs[-6:]
    t = pl.program_id(0)
    half = head // 2
    scale = head**-0.5

    @pl.when(t == 0)
    def _():
        win[:WINDOW] = prev[...]
        win[WINDOW:] = cur[...]

    pre = dot(normed[...], wq[...], 1, 0)
    cos, sin = cos_r[...], sin_r[...]
    for h in range(heads):
        a = pre[:, h * head : h * head + half]
        b = pre[:, h * head + half : (h + 1) * head]
        q_o[h * TILE : (h + 1) * TILE, :half] = (a * cos - b * sin).astype(BF)
        q_o[h * TILE : (h + 1) * TILE, half:] = (b * cos + a * sin).astype(BF)
    window = pl.ds(pl.multiple_of(t * TILE, TILE), SPAN)
    keys = win[window, :head]
    values = win[window, head:]
    k_at = lax.broadcasted_iota(jnp.int32, (TILE, SPAN), 1)
    q_at = lax.broadcasted_iota(jnp.int32, (TILE, SPAN), 0)
    k_base = first[0] + (base + t) * TILE - WINDOW
    low = meta[:, 2:3].astype(jnp.int32) - k_base
    allowed = (k_at >= low) & (k_at <= q_at + WINDOW)
    for h in range(heads):
        rows = slice(h * TILE, (h + 1) * TILE)
        scores = jnp.where(allowed, dot(q_o[rows], keys, 1, 1) * scale, -1e30)
        top = jnp.max(scores, axis=1, keepdims=True)
        e = jnp.exp(scores - top)
        total = jnp.sum(e, axis=1, keepdims=True)
        probs = (e * (1.0 / total)).astype(BF)
        p_o[rows] = probs
        ctx_o[:, h * head : (h + 1) * head] = dot(probs, values, 1, 0).astype(BF)
    mid = tok[...].astype(F32) + dot(ctx_o[...], wo[...], 1, 0)
    mid_o[...] = mid
    root = lax.rsqrt(jnp.mean(mid * mid, axis=1, keepdims=True) + EPS)
    nf_o[...] = (mid * root * gain[...]).astype(BF)


def ffn_kernel(nf, cot, meta, mid, gain, wg, wu, wd, act_o, dg_o, du_o, db_o, mixed_o, dh_o, da_o, gg_o, out, dn):
    j = pl.program_id(0)

    @pl.when(j == 0)
    def _():
        out[...] = jnp.zeros_like(out)
        dn[...] = jnp.zeros_like(dn)
        db_o[...] = (cot[...].astype(F32) * meta[:, 1:2]).astype(BF)

    x, db = nf[...], db_o[...]
    gate = dot(x, wg[...], 1, 0)
    up = dot(x, wu[...], 1, 0)
    sig = 1.0 / (1.0 + jnp.exp(-gate))
    gs = gate * sig
    act = (gs * up).astype(BF)
    act_o[...] = act
    out[...] += dot(act, wd[...], 1, 0)
    d_act = dot(db, wd[...], 1, 1)
    d_up = (d_act * gs).astype(BF)
    d_gate = (d_act * up * sig * (1.0 + gate * (1.0 - sig))).astype(BF)
    du_o[...] = d_up
    dg_o[...] = d_gate
    dn[...] += dot(d_gate, wg[...], 1, 1) + dot(d_up, wu[...], 1, 1)

    @pl.when(j == pl.num_programs(0) - 1)
    def _():
        total = jnp.zeros(gg_o.shape, F32)
        for i in range(mid.shape[0] // TILE):
            r = slice(i * TILE, (i + 1) * TILE)
            v = mid[r]
            live = meta[r, 1:2]
            mixed_o[r] = ((v + out[r]) * live).astype(BF)
            root = lax.rsqrt(jnp.mean(v * v, axis=1, keepdims=True) + EPS)
            g = dn[r]
            total = total + jnp.sum(g * v * root, axis=0, keepdims=True)
            w = g * gain[...]
            mean = jnp.mean(w * v, axis=1, keepdims=True)
            d = db_o[r].astype(F32) + root * w - v * (root * root * root) * mean
            dh_o[r] = d
            da_o[r] = d.astype(BF)
        gg_o[...] = total


def put_columns(ref, at, value):
    rows = value.shape[0]
    for k in range(value.shape[1] // 128):
        ref[at + k * rows : at + (k + 1) * rows] = value[:, k * 128 : (k + 1) * 128]


def take_columns(ref, at, rows, count):
    return jnp.concatenate(
        [ref[at + k * rows : at + (k + 1) * rows].astype(F32) for k in range(count)], axis=1
    )


def weights_kernel(with_out, adding, *refs):
    (_, act, dg, du, nf, db) = refs[:6]
    at = 6
    if with_out:
        ctx, da = refs[at : at + 2]
        at += 2
    if adding:
        received = refs[at]
    out, acc = refs[-2:]
    x = nf[...]
    width = x.shape[1]
    size = width * HB // 128
    put_columns(acc, 0, dot(x, dg[...], 0, 0))
    put_columns(acc, size, dot(x, du[...], 0, 0))
    put_columns(acc, 2 * size, dot(act[...], db[...], 0, 0))
    if with_out:
        put_columns(acc, 3 * size, dot(ctx[...], da[...], 0, 0))
    if adding:
        out[...] = (acc[...] + received[...].astype(F32)).astype(BF)
    else:
        out[...] = acc[...].astype(BF)


def unrotate(a, b, cos, sin):
    return a * cos + b * sin, b * cos - a * sin


def attend_back_kernel(upper, heads, head, *refs):
    (da, wo, p_r, q_r, prev, cur, cos_r, sin_r) = refs[:8]
    at = 8
    if upper:
        (low_cur, cos_l, sin_l, _) = refs[8:12]
        (dq_o, pair_o, cur_o, win, acc, dctx, ds) = refs[-7:]
    else:
        (dq_o, prev_o, cur_o, win, acc, dctx, ds) = refs[-7:]
    t = pl.program_id(0)
    half = head // 2
    scale = head**-0.5

    @pl.when(t == 0)
    def _():
        win[:WINDOW] = prev[...]
        win[WINDOW:] = cur[...]
        if upper:
            acc[:WINDOW] = low_cur[...]
        else:
            acc[:WINDOW] = jnp.zeros((WINDOW, 2 * head), F32)
        acc[WINDOW:] = jnp.zeros((WINDOW, 2 * head), F32)

    d_ctx = dot(da[...], wo[...], 1, 1).astype(BF)
    for h in range(heads):
        dctx[h * TILE : (h + 1) * TILE] = d_ctx[:, h * head : (h + 1) * head]
    window = pl.ds(pl.multiple_of(t * TILE, TILE), SPAN)
    keys = win[window, :head]
    values = win[window, head:]
    for h in range(heads):
        rows = slice(h * TILE, (h + 1) * TILE)
        d_probs = dot(dctx[rows], values, 1, 1)
        probs = p_r[rows].astype(F32)
        both = probs * d_probs
        total = jnp.sum(both, axis=1, keepdims=True)
        ds[rows] = (both - probs * total).astype(BF)
    cos, sin = cos_r[...], sin_r[...]
    for h in range(heads):
        rows = slice(h * TILE, (h + 1) * TILE)
        dq = dot(ds[rows], keys, 1, 0) * scale
        a, b = unrotate(dq[:, :half], dq[:, half:], cos, sin)
        dq_o[:, h * head : h * head + half] = a.astype(BF)
        dq_o[:, h * head + half : (h + 1) * head] = b.astype(BF)
    acc[window, :head] += dot(ds[...], q_r[...], 0, 0) * scale
    acc[window, head:] += dot(p_r[...], dctx[...], 0, 0)

    @pl.when(t == pl.num_programs(0) - 1)
    def _():
        cur_o[...] = acc[WINDOW:]
        if upper:
            a, b = unrotate(acc[:WINDOW, :half], acc[:WINDOW, half:head], cos_l[...], sin_l[...])
            pair_o[:, :half] = a.astype(BF)
            pair_o[:, half:head] = b.astype(BF)
            pair_o[:, head:] = acc[:WINDOW, head:].astype(BF)
        else:
            prev_o[...] = acc[:WINDOW].astype(BF)


def pair_kernel(head, cur, back, cos_r, sin_r, _, pair_o):
    half = head // 2
    d = cur[...] + back[...].astype(F32)
    a, b = unrotate(d[:, :half], d[:, half:head], cos_r[...], sin_r[...])
    pair_o[:, :half] = a.astype(BF)
    pair_o[:, half:head] = b.astype(BF)
    pair_o[:, head:] = d[:, head:].astype(BF)


def input_kernel(dq, dp, wq, wkv, tok, meta, gain, dh, grad_o, gg_o):
    j = pl.program_id(0)
    dn = dot(dq[...], wq[...], 1, 1) + dot(dp[...], wkv[...], 1, 1)
    v = tok[...].astype(F32)
    root = meta[:, 0:1]
    part = jnp.sum(dn * v * root, axis=0, keepdims=True)

    @pl.when(j == 0)
    def _():
        gg_o[...] = part

    @pl.when(j != 0)
    def _():
        gg_o[...] += part

    w = dn * gain[...]
    mean = jnp.mean(w * v, axis=1, keepdims=True)
    grad_o[...] = dh[...] + root * w - v * (root * root * root) * mean


GAIN_ROWS = 128


def project_kernel(adding, *refs):
    (_, normed, dq, dp) = refs[:4]
    out, acc = refs[-2:]
    x = normed[...]
    width = x.shape[1]
    at_kv = width * dq.shape[1] // 128
    at_gain = at_kv + width * dp.shape[1] // 128
    put_columns(acc, 0, dot(x, dq[...], 0, 0))
    put_columns(acc, at_kv, dot(x, dp[...], 0, 0))
    acc[at_gain:] = jnp.zeros((GAIN_ROWS, 128), F32)
    if adding:
        received, g_attn, g_ffn = refs[4:7]
        for k in range(width // 128):
            lanes = slice(k * 128, (k + 1) * 128)
            acc[at_gain + k : at_gain + k + 1] = g_attn[:, lanes]
            acc[at_gain + 8 + k : at_gain + 9 + k] = g_ffn[:, lanes]
        out[...] = (acc[...] + received[...].astype(F32)).astype(BF)
    else:
        out[...] = acc[...].astype(BF)


def finish_ffn_kernel(with_out, *refs):
    flat = refs[1]
    outs = refs[-3:] if with_out else refs[-2:]
    gate_o, down_o = outs[:2]
    width = gate_o.shape[0]
    size = width * HB // 128
    u = pl.program_id(1)

    @pl.when(u == 0)
    def _():
        gate_o[...] = take_columns(flat, 0, width, HB // 128)
        down_o[...] = take_columns(flat, 2 * size, HB, width // 128)
        if with_out:
            outs[2][...] = take_columns(flat, 3 * size, HB, width // 128)

    @pl.when(u != 0)
    def _():
        gate_o[...] = take_columns(flat, size, width, HB // 128)


def finish_project_kernel(last, *refs):
    flat = refs[1]
    q_o, kv_o, g_attn, g_ffn = refs[-4:]
    width = q_o.shape[0]
    at_kv = width * q_o.shape[1] // 128
    at_gain = at_kv + width * kv_o.shape[1] // 128
    q_o[...] = take_columns(flat, 0, width, q_o.shape[1] // 128)
    kv_o[...] = take_columns(flat, at_kv, width, kv_o.shape[1] // 128)
    for k in range(width // 128):
        lanes = slice(k * 128, (k + 1) * 128)
        a = flat[at_gain : at_gain + 8].astype(F32)[k : k + 1]
        f = flat[at_gain + 8 : at_gain + 16].astype(F32)[k : k + 1]
        if last:
            a = a + refs[2][:, lanes]
            f = f + refs[3][:, lanes]
        g_attn[:, lanes] = a
        g_ffn[:, lanes] = f


def swap_cores(value):
    return lax.ppermute(value, "core", [(0, 1), (1, 0)])


def exchange(value, axes):
    return lax.all_to_all(value, axes, 0, 0, tiled=True)


PLANE = ("hi", "near")
LINE = ("far",)


def summed_everywhere(flat, order):
    value = flat
    shape = value.shape
    for at, axes in enumerate(order):
        n = math.prod(lax.axis_size(a) for a in axes)
        parts = exchange(value, axes).reshape(n, -1, 128)
        value = jnp.sum(parts.astype(F32), axis=0).astype(BF)
    for axes in reversed(order):
        n = math.prod(lax.axis_size(a) for a in axes)
        value = exchange(jnp.broadcast_to(value[None], (n,) + value.shape), axes).reshape(-1, 128)
    return value.reshape(shape)


def per_device(tokens, lengths, gain_attn, w_query, w_keyvalue, w_out, gain_ffn, w_gate_up, w_down, cotangent):
    rows, width = tokens.shape
    head = w_keyvalue.shape[1] // 2
    heads = w_query.shape[1] // head
    hidden = w_down.shape[0]
    half = head // 2
    tiles = rows // TILE
    per = WINDOW // TILE
    hq = heads * head
    seq = ("far", "near")
    seq_index = lax.axis_index(seq)
    seq_count = lax.axis_size(seq)
    core = lax.axis_index("core")
    first = (seq_index * rows).astype(jnp.int32).reshape(1)
    mine = core.astype(jnp.int32).reshape(1)
    other = (1 - core).astype(jnp.int32).reshape(1)
    gain_a = gain_attn.reshape(1, width)
    gain_f = gain_ffn.reshape(1, width)

    def row_block(cols):
        return pl.BlockSpec((TILE, cols), lambda i, *_: (i, 0))

    tail_from = tiles - per
    normed, kv, tail, cos, sin, meta = call(
        pre_kernel,
        "pre",
        (tiles,),
        [row_block(width), whole(lengths.shape), whole((1, width)), whole(w_keyvalue.shape)],
        [
            row_block(width),
            row_block(2 * head),
            pl.BlockSpec((TILE, 2 * head), lambda i, *_: (jnp.maximum(i - tail_from, 0), 0)),
            row_block(half),
            row_block(half),
            row_block(128),
        ],
        [
            sds((rows, width), BF),
            sds((rows, 2 * head), BF),
            sds((WINDOW, 2 * head), BF),
            sds((rows, half), F32),
            sds((rows, half), F32),
            sds((rows, 128), F32),
        ],
        scalars=1,
        flops=2 * rows * width * 2 * head + 2**25,
        nbytes=6 * 2**20,
    )(first, tokens, lengths, gain_a, w_keyvalue)
    halo = lax.ppermute(tail, seq, [(i, i + 1) for i in range(seq_count - 1)])

    blocks = rows // WINDOW
    attend_shapes = [
        sds((heads * rows, head), BF),
        sds((heads * rows, SPAN), BF),
        sds((rows, hq), BF),
        sds((rows, width), F32),
        sds((rows, width), BF),
    ]
    attend_flops = 2 * WINDOW * (2 * width * hq + heads * 2 * SPAN * head)
    state = None
    for block in reversed(range(blocks)):
        base = block * per

        def at(cols, r=TILE, base=base):
            return pl.BlockSpec((r, cols), lambda i, *_: (base + i, 0))

        prev = halo if block == 0 else kv
        prev_at = max(block - 1, 0)
        ins = [
            at(width),
            at(width),
            at(half),
            at(half),
            at(128),
            pl.BlockSpec((WINDOW, 2 * head), lambda i, *_, b=prev_at: (b, 0)),
            pl.BlockSpec((WINDOW, 2 * head), lambda i, *_, b=block: (b, 0)),
            whole(w_query.shape),
            whole(w_out.shape),
            whole((1, width)),
        ]
        args = [first, normed, tokens, cos, sin, meta, prev, kv, w_query, w_out, gain_f]
        aliases = {}
        if state is not None:
            aliases = {len(args) + i: i for i in range(5)}
            args += state
            ins += [anywhere()] * 5
        state = call(
            functools.partial(attend_kernel, base, heads, head),
            f"attend{block}",
            (per,),
            ins,
            [at(head, heads * TILE), at(SPAN, heads * TILE), at(hq), at(width), at(width)],
            attend_shapes,
            scratch=[pltpu.VMEM((2 * WINDOW, 2 * head), BF)],
            scalars=1,
            aliases=aliases,
            flops=attend_flops,
            nbytes=8 * 2**20,
        )(*args)
    queries, probs, context, hidden_mid, normed_ffn = state

    steps = hidden // HB

    def hidden_block():
        return pl.BlockSpec((rows, HB), lambda j, *_: (0, j))

    act, d_gate, d_up, d_branch, mixed, d_hidden, d_attn, grad_gain_f = call(
        ffn_kernel,
        "ffn",
        (steps,),
        [
            whole((rows, width)),
            whole((rows, width)),
            whole((rows, 128)),
            whole((rows, width)),
            whole((1, width)),
            pl.BlockSpec((width, HB), lambda j: (0, j)),
            pl.BlockSpec((width, HB), lambda j: (0, j + steps)),
            pl.BlockSpec((HB, width), lambda j: (j, 0)),
        ],
        [hidden_block()] * 3
        + [whole((rows, width))] * 4
        + [whole((1, width))],
        [sds((rows, hidden), BF)] * 3
        + [sds((rows, width), BF), sds((rows, width), BF), sds((rows, width), F32), sds((rows, width), BF)]
        + [sds((1, width), F32)],
        scratch=[pltpu.VMEM((rows, width), F32), pltpu.VMEM((rows, width), F32)],
        flops=2 * rows * width * hidden * 6,
        nbytes=32 * 2**20,
    )(normed_ffn, cotangent, meta, hidden_mid, gain_f, w_gate_up, w_gate_up, w_down)

    size = width * HB // 128
    own_blocks = steps // 2
    per_chunk = own_blocks // 2

    def weights(chunk, owner, received):
        with_out = chunk == 1
        unit = size * (4 if with_out else 3)

        def hid(j, o):
            return (0, o[0] * own_blocks + chunk * per_chunk + j)

        ins = [pl.BlockSpec((rows, HB), hid)] * 3 + [whole((rows, width))] * 2
        args = [owner, act, d_gate, d_up, normed_ffn, d_branch]
        if with_out:
            ins += [
                pl.BlockSpec((rows, HB), lambda j, o: (0, o[0] * per_chunk + j)),
                whole((rows, width)),
            ]
            args += [context, d_attn]
        if received is not None:
            ins.append(pl.BlockSpec((unit, 128), lambda j, o: (j, 0)))
            args.append(received)
        return call(
            functools.partial(weights_kernel, with_out, received is not None),
            f"weights{chunk}{'add' if received is not None else 'give'}",
            (per_chunk,),
            ins,
            pl.BlockSpec((unit, 128), lambda j, o: (j, 0)),
            sds((per_chunk * unit, 128), BF),
            scratch=[pltpu.VMEM((unit, 128), F32)],
            scalars=1,
            flops=2 * rows * width * HB * per_chunk * (4 if with_out else 3),
            nbytes=8 * 2**20,
        )(*args)

    given0 = swap_cores(weights(0, other, None))
    given1 = swap_cores(weights(1, other, None))
    half0 = weights(0, mine, given0)
    total0 = summed_everywhere(half0, (PLANE, LINE))
    half1 = weights(1, mine, given1)
    total1 = summed_everywhere(half1, (PLANE, LINE))

    back_flops = 2 * WINDOW * (width * hq + heads * 4 * SPAN * head)
    back_scratch = [
        pltpu.VMEM((2 * WINDOW, 2 * head), BF),
        pltpu.VMEM((2 * WINDOW, 2 * head), F32),
        pltpu.VMEM((heads * TILE, head), BF),
        pltpu.VMEM((heads * TILE, SPAN), BF),
    ]
    dq, carried, sent = None, None, None
    pair = None
    for block in range(blocks):
        base = block * per
        upper = block > 0

        def at(cols, r=TILE, base=base):
            return pl.BlockSpec((r, cols), lambda i, *_: (base + i, 0))

        def spans(cols, b):
            return pl.BlockSpec((WINDOW, cols), lambda i, *_: (b, 0))

        prev = halo if block == 0 else kv
        prev_at = max(block - 1, 0)
        args = [d_attn, w_out, probs, queries, prev, kv, cos, sin]
        ins = [
            at(width),
            whole(w_out.shape),
            at(SPAN, heads * TILE),
            at(head, heads * TILE),
            spans(2 * head, prev_at),
            spans(2 * head, block),
            at(half),
            at(half),
        ]
        if upper:
            args += [carried, cos, sin, dq]
            ins += [whole((WINDOW, 2 * head)), spans(half, prev_at), spans(half, prev_at), anywhere()]
            aliases = {11: 0}
            outs = [at(hq), spans(2 * head, prev_at), whole((WINDOW, 2 * head))]
            shapes = [sds((rows, hq), BF), sds((rows, 2 * head), BF), sds((WINDOW, 2 * head), F32)]
            if pair is not None:
                args.append(pair)
                ins.append(anywhere())
                aliases[12] = 1
        else:
            aliases = {}
            outs = [at(hq), whole((WINDOW, 2 * head)), whole((WINDOW, 2 * head))]
            shapes = [sds((rows, hq), BF), sds((WINDOW, 2 * head), BF), sds((WINDOW, 2 * head), F32)]
        dq, second, carried = call(
            functools.partial(attend_back_kernel, upper, heads, head),
            f"back{block}",
            (per,),
            ins,
            outs,
            shapes,
            scratch=back_scratch,
            aliases=aliases,
            flops=back_flops,
            nbytes=8 * 2**20,
        )(*args)
        if upper:
            pair = second
        else:
            sent = lax.ppermute(second, seq, [(i + 1, i) for i in range(seq_count - 1)])

    end = blocks - 1
    pair = call(
        functools.partial(pair_kernel, head),
        "pair",
        (1,),
        [
            whole((WINDOW, 2 * head)),
            whole((WINDOW, 2 * head)),
            pl.BlockSpec((WINDOW, half), lambda i: (end, 0)),
            pl.BlockSpec((WINDOW, half), lambda i: (end, 0)),
            anywhere(),
        ],
        pl.BlockSpec((WINDOW, 2 * head), lambda i: (end, 0)),
        sds((rows, 2 * head), BF),
        aliases={4: 0},
        flops=2**22,
        nbytes=3 * 2**20,
    )(carried, sent, cos, sin, pair)

    q_cols, kv_cols = hq // 2, head
    flat2 = width * (q_cols + kv_cols) // 128 + GAIN_ROWS

    def project(owner, extra):
        ins = [
            whole((rows, width)),
            pl.BlockSpec((rows, q_cols), lambda i, o: (0, o[0])),
            pl.BlockSpec((rows, kv_cols), lambda i, o: (0, o[0])),
        ]
        args = [owner, normed, dq, pair]
        if extra:
            ins += [whole((flat2, 128)), whole((1, width)), whole((1, width))]
            args += extra
        return call(
            functools.partial(project_kernel, bool(extra)),
            f"project{'add' if extra else 'give'}",
            (1,),
            ins,
            whole((flat2, 128)),
            sds((flat2, 128), BF),
            scratch=[pltpu.VMEM((flat2, 128), F32)],
            scalars=1,
            flops=2 * rows * width * (q_cols + kv_cols),
            nbytes=5 * 2**20,
        )(*args)

    given2 = swap_cores(project(other, None))
    input_grad, grad_gain_a = call(
        input_kernel,
        "input",
        (tiles,),
        [
            row_block(hq),
            row_block(2 * head),
            whole(w_query.shape),
            whole(w_keyvalue.shape),
            row_block(width),
            row_block(128),
            whole((1, width)),
            row_block(width),
        ],
        [row_block(width), whole((1, width))],
        [sds((rows, width), F32), sds((1, width), F32)],
        flops=2 * rows * width * (hq + 2 * head),
        nbytes=14 * 2**20,
    )(dq, pair, w_query, w_keyvalue, tokens, meta, gain_a, d_hidden)
    half2 = project(mine, [given2, grad_gain_a, grad_gain_f])
    total2 = summed_everywhere(half2, (PLANE, LINE))

    def finish_ffn(chunk, owner, flat, state):
        with_out = chunk == 1
        unit = size * (4 if with_out else 3)

        def block_of(j, o):
            return o[0] * own_blocks + chunk * per_chunk + j

        outs = [
            pl.BlockSpec((width, HB), lambda j, u, o: (0, block_of(j, o) + u * steps)),
            pl.BlockSpec((HB, width), lambda j, u, o: (block_of(j, o), 0)),
        ]
        shapes = [sds((width, 2 * hidden), F32), sds((hidden, width), F32)]
        if with_out:
            outs.append(pl.BlockSpec((HB, width), lambda j, u, o: (o[0] * per_chunk + j, 0)))
            shapes.append(sds((hq, width), F32))
        args = [owner, flat]
        ins = [pl.BlockSpec((unit, 128), lambda j, u, o: (j, 0))]
        aliases = {2 + i: i for i in range(len(state))}
        return call(
            functools.partial(finish_ffn_kernel, with_out),
            f"finish{chunk}",
            (per_chunk, 2),
            ins + [anywhere()] * len(state),
            outs,
            shapes,
            scalars=1,
            aliases=aliases,
            flops=2**22,
            nbytes=6 * 2**20,
        )(*args, *state)

    done = finish_ffn(0, mine, total0, [])
    done = finish_ffn(0, other, swap_cores(total0), list(done))
    done = finish_ffn(1, mine, total1, list(done))
    grad_gate_up, grad_down, grad_out = finish_ffn(1, other, swap_cores(total1), list(done))

    def finish_project(owner, flat, state, gains):
        last = bool(state)
        ins = [whole((flat2, 128))]
        args = [owner, flat]
        aliases = {}
        if last:
            ins += [whole((1, width))] * 2 + [anywhere()] * 2
            args += gains + state
            aliases = {4: 0, 5: 1}
        return call(
            functools.partial(finish_project_kernel, last),
            "finish2",
            (1,),
            ins,
            [
                pl.BlockSpec((width, q_cols), lambda i, o: (0, o[0])),
                pl.BlockSpec((width, kv_cols), lambda i, o: (0, o[0])),
                whole((1, width)),
                whole((1, width)),
            ],
            [
                sds((width, hq), F32),
                sds((width, 2 * head), F32),
                sds((1, width), F32),
                sds((1, width), F32),
            ],
            scalars=1,
            aliases=aliases,
            flops=2**22,
            nbytes=3 * 2**20,
        )(*args)

    gq, gkv, ga, gf = finish_project(mine, total2, [], [])
    gq, gkv, ga, gf = finish_project(other, swap_cores(total2), [gq, gkv], [ga, gf])
    return (
        mixed,
        input_grad,
        kv,
        ga.reshape(width),
        gq,
        gkv,
        grad_out,
        gf.reshape(width),
        grad_gate_up,
        grad_down,
    )


def solution(mesh):
    outer, seq = mesh.devices.shape if hasattr(mesh, "devices") else (mesh.shape["outer"], mesh.shape["seq"])
    fine = Mesh(
        mesh.devices.reshape(outer // 2, 2, seq // 2, 2), ("hi", "core", "far", "near")
    )
    everywhere = ("hi", "core", "far", "near")
    rows = P(everywhere, None)
    return jax.shard_map(
        per_device,
        mesh=fine,
        in_specs=(rows, P(("hi", "core"), None)) + (P(),) * 7 + (rows,),
        out_specs=(rows,) * 3 + (P(),) * 7,
        check_vma=False,
    )
```
